128 devices in a mesh: dp: 16 (over x, z), mp: 8 (over y, core).
Axes of the slice: x: 4, y: 4, z: 4, core: 2. Of those that a mesh axis runs over, the one named last changes fastest.
Arguments:
- context: bfloat16 [4096, 4096], P('dp', 'mp'), may hold values from -6 to 6
- w_out: bfloat16 [4096, 8192], P('mp'), may hold values from -0.09375 to 0.09375
- residual: bfloat16 [4096, 8192], P('dp', 'mp'), may hold values from -6 to 6
- norm_gain: float32 [8192], P('mp'), may hold values from 0.25 to 1.75
- w_join: bfloat16 [8192, 4096], P('mp'), may hold values from -0.0625 to 0.0625
- dec_state: bfloat16 [6144, 4096], P('dp', 'mp'), may hold values from -6 to 6
- gate_s: float32 [4096], P('mp'), may hold values from -1 to 1
- gate_h: float32 [4096], P('mp'), may hold values from 0.5 to 2
- gate_bias: float32 [4096], P('mp'), may hold values from -1 to 1
- owner: int32 [4096, 1], P('dp'), may hold values from 0 to 15; in each aligned block of 256 rows (0 to 255, 256 to 511, ...) at most 24 rows name the same one
- pad_mask: int32 [4096], P('dp'), may hold values 0 or 1
- cotangent: bfloat16 [6144, 4096], P('dp', 'mp'), may hold values from -6 to 6
Outputs:
- joined: bfloat16 [6144, 4096], P('dp', 'mp')
- state_grad: bfloat16 [6144, 4096], P('dp', 'mp')
- join_grad: float32 [8192, 4096], P('mp', 'dp')
The draws below stay inside these ranges and needn't reach their ends.
Inputs may be any that keep to these rules, and one draw needn't show every extreme that they name: `owner`: within each shard of 256 tokens no pair group is named more than 24 times, and in some shard one group is named exactly 24 times.
All inputs are finite; a program needn't handle non-finite values. No bound on the sum of `pad_mask` on one device may be relied on, other than what follows from the above.
Results may differ from the reference program's by a relative error of at most 0.02.
Values may be sent and summed in bfloat16 or wider, within the bound.
No kernel may reach another device: no remote copies, remote signals or barrier semaphores. Data moves between devices by JAX's collectives and lax.ppermute only.
A program may use at most 128 MiB of HBM per device.

```python
import math
import jax
import jax.numpy as jnp
import numpy as np
from jax import lax

HQ = 4096
DL = 8192
DT = 4096
TOK_DEV = 256
TOKENS = 4096
MOST = 24
CAP = 384
N_DP = 16
N_MP = 8


def plant(result, own_key, low, largest):
    longest = result.shape.index(max(result.shape))
    spots = []
    for shift in (0, 1):
        where = [jax.random.randint(jax.random.fold_in(own_key, axis), (), 0, length) for axis, length in enumerate(result.shape)]
        where[longest] = (where[longest] + shift) % result.shape[longest]
        spots.append(tuple(where))
    return result.at[spots[0]].set(low).at[spots[1]].set(largest)


def block_levels(rng, dims, shards, least, largest):
    level = 1.0
    for axis_at, parts in shards:
        steps = jax.random.uniform(jax.random.fold_in(jax.random.fold_in(rng, 6), axis_at), (parts,), jnp.float32, least / len(shards), largest / len(shards))
        level = level * jnp.repeat(jnp.exp(steps), dims[axis_at] // parts).reshape((-1,) + (1,) * (len(dims) - 1 - axis_at))
    return level


def assign_block(own_key, own, number, rows, count, top, limit, lean):
    order = jax.random.permutation(own_key, count)
    packed, ordinary = load_shares(count, rows * top, limit, lean, True), load_shares(count, rows * top, limit, lean, False)
    places = jnp.arange(count)

    def named(lengths, turn):
        used = int((lengths > 0).sum())
        fixed = max(1, used // 4)
        shifted = fixed + (places - fixed + turn * (used - fixed)) % max(1, count - fixed)
        return jnp.zeros((count,), jnp.int32).at[order[jnp.where(places < fixed, places, shifted)]].set(jnp.asarray(lengths, jnp.int32))

    lengths = jnp.where(number % 4 == 0, named(packed, number // 4), named(ordinary, number - number // 4 - 1))
    mixed = jax.random.permutation(jax.random.fold_in(own, 3), count)
    giver, taker = mixed[0:count // 2 * 2:2], mixed[1:count // 2 * 2:2]
    slack = jnp.minimum(lengths[giver] - 1, limit - lengths[taker]) // 2
    slack = jnp.where((giver == order[0]) | (taker == order[0]) | (lengths[taker] == 0), 0, jnp.maximum(slack, 0))
    shifted = jax.random.randint(jax.random.fold_in(own, 4), (count // 2,), 0, 1 << 20) % (slack + 1)
    lengths = lengths.at[giver].add(-shifted).at[taker].add(shifted)
    members = jnp.searchsorted(jnp.cumsum(lengths), jnp.arange(rows * top), side="right").astype(jnp.int32)
    listing = members.reshape(top, rows).T
    listing = listing[jax.random.permutation(jax.random.fold_in(own, 1), rows)]
    turn = jax.random.randint(jax.random.fold_in(own, 2), (rows, 1), 0, top)
    return jnp.take_along_axis(listing, (jnp.arange(top)[None, :] + turn) % top, axis=1)


def load_shares(count, total, most, skew, full):
    weights = [(1 << 20) // math.isqrt(rank ** skew) + 1 for rank in range(1, count + 1)]
    largest = most if full else min(most, max(-(-total // count), total * weights[0] // sum(weights)))
    least = 1 if total - largest >= count - 1 else 0
    counts, spare = [largest] + [least] * (count - 1), total - largest - least * (count - 1)
    while spare > 0:
        free = [i for i in range(1, count) if counts[i] < largest] or [i for i in range(1, count) if counts[i] < most]
        pool, left = sum([weights[i] for i in free]), spare
        for i in free:
            extra = min(most - counts[i], max(1, left * weights[i] // pool), spare)
            counts[i] = counts[i] + extra
            spare = spare - extra
    return np.array(counts)


def centred(rng, shape, deviation, reach, split=(), held_as=jnp.bfloat16):
    values = jax.random.normal(rng, shape, jnp.float32) * deviation
    if len(split) > 0:
        values = block_levels(rng, shape, split, -0.22, 0.18) * values
    return jnp.clip(values, min=-reach, max=reach).astype(held_as)


def setup_inputs(seed: int = 0) -> dict:
    arg_keys = jax.random.split(jax.random.key(seed), 13)
    context = centred(arg_keys[0], (TOKENS, HQ), 1.0, 6.0, ((0, 16), (1, 8)))
    w_out = centred(arg_keys[1], (HQ, DL), HQ ** -0.5, 0.09375, ((0, 8),))
    residual = centred(arg_keys[2], (TOKENS, DL), 1.0, 6.0, ((0, 16), (1, 8)))
    norm_gain = jnp.clip(1.0 + 0.15 * jax.random.normal(arg_keys[3], (DL,), jnp.float32), 0.25, 1.75)
    w_join = centred(arg_keys[4], (DL, DT), DL ** -0.5, 0.0625, ((0, 8),))
    dec_state = centred(arg_keys[5], (N_DP * CAP, DT), 1.0, 6.0, ((0, 16), (1, 8)))
    gate_s = jnp.clip(jax.random.uniform(arg_keys[6], (DT,), jnp.float32, -1.0, 1.0) * block_levels(arg_keys[6], (DT,), ((0, 8),), -0.4, 0.0), -1.0, 1.0)
    gate_h = jnp.clip(0.5 + 1.5 * jax.random.uniform(arg_keys[7], (DT,), jnp.float32) ** block_levels(arg_keys[7], (DT,), ((0, 8),), -0.2, 0.2), 0.5, 2.0)
    gate_bias = jnp.clip(jax.random.uniform(arg_keys[8], (DT,), jnp.float32, -1.0, 1.0) * block_levels(arg_keys[8], (DT,), ((0, 8),), -0.4, 0.0), -1.0, 1.0)
    owner_keys = jax.random.split(jax.random.fold_in(arg_keys[9], 1), TOKENS // TOK_DEV)
    owner_turns = jax.random.permutation(jax.random.fold_in(arg_keys[9], 3), TOKENS // TOK_DEV)
    owner = jax.vmap(lambda own, number: assign_block(jax.random.fold_in(arg_keys[9], 2), own, number, TOK_DEV, N_DP, 1, MOST, 2))(owner_keys, owner_turns).reshape((TOKENS, 1))
    pad_mask = plant((jax.random.randint(arg_keys[10], (TOKENS,), 0, 4) < 3).astype(jnp.int32), jax.random.fold_in(arg_keys[10], 1), 0, 1)
    cotangent = centred(arg_keys[11], (N_DP * CAP, DT), 1.0, 6.0, ((0, 16), (1, 8)))
    return dict(context=context, w_out=w_out, residual=residual, norm_gain=norm_gain, w_join=w_join, dec_state=dec_state, gate_s=gate_s, gate_h=gate_h, gate_bias=gate_bias, owner=owner, pad_mask=pad_mask, cotangent=cotangent)


def reference(context, w_out, residual, norm_gain, w_join, dec_state, gate_s, gate_h, gate_bias, owner, pad_mask, cotangent):
    heads = HQ // N_MP
    summed = jnp.zeros((TOKENS, DL), jnp.float32)
    for group in range(N_MP):
        term = jnp.dot(context[:, group * heads:(group + 1) * heads], w_out[group * heads:(group + 1) * heads], preferred_element_type=jnp.float32)
        summed = summed + lax.optimization_barrier(term.astype(jnp.bfloat16)).astype(jnp.float32)
    mixed = residual.astype(jnp.float32) + summed
    scale = lax.rsqrt(lax.optimization_barrier(jnp.mean(mixed * mixed, axis=1)) + 1e-05)
    normed = (mixed * scale[:, None] * norm_gain.astype(jnp.float32)[None, :] * pad_mask.astype(jnp.float32)[:, None]).astype(jnp.bfloat16)
    target = owner[:, 0].astype(jnp.int32).reshape(N_DP, TOK_DEV)
    onehot = (target[:, :, None] == jnp.arange(N_DP, dtype=jnp.int32)[None, None, :]).astype(jnp.int32)
    before = jnp.cumsum(onehot, axis=1) - onehot
    rank = lax.optimization_barrier(jnp.sum(before * onehot, axis=2)).astype(jnp.int32)
    source = jnp.arange(N_DP, dtype=jnp.int32)[:, None]
    slots = (target * CAP + source * MOST + rank).reshape(TOKENS).astype(jnp.int32)
    placed = jnp.zeros((N_DP * CAP, DL), jnp.bfloat16).at[slots].set(normed)
    rows = DL // N_MP
    hidden = jnp.zeros((N_DP * CAP, DT), jnp.float32)
    for group in range(N_MP):
        term = jnp.dot(placed[:, group * rows:(group + 1) * rows], w_join[group * rows:(group + 1) * rows], preferred_element_type=jnp.float32)
        hidden = hidden + lax.optimization_barrier(term.astype(jnp.bfloat16)).astype(jnp.float32)
    state = dec_state.astype(jnp.float32)
    gate = jax.nn.sigmoid(gate_s[None, :] * state + gate_h[None, :] * hidden + gate_bias[None, :])
    joined = (state + gate * hidden).astype(jnp.bfloat16)
    outer = cotangent.astype(jnp.float32)
    slope = gate * (1.0 - gate) * hidden
    hidden_grad = (outer * (gate + slope * gate_h[None, :])).astype(jnp.bfloat16)
    state_grad = (outer * (1.0 + slope * gate_s[None, :])).astype(jnp.bfloat16)
    join_grad = jnp.dot(placed.T, hidden_grad, preferred_element_type=jnp.float32)
    return (joined, state_grad, join_grad)
```

```python
import jax
import jax.numpy as jnp
from jax import lax
from jax.sharding import Mesh, PartitionSpec as P

AXES = ("x", "z", "y", "c")
N = 4
BF = jnp.bfloat16
F32 = jnp.float32


def move(value, where):
    pairs = []
    for x in range(N):
        for z in range(N):
            for y in range(N):
                for c in range(2):
                    tx, tz, ty, tc = where(x, z, y, c)
                    pairs.append(
                        (
                            ((x * N + z) * N + y) * 2 + c,
                            (((tx % N) * N + tz % N) * N + ty % N) * 2 + tc % 2,
                        )
                    )
    return lax.ppermute(value, AXES, pairs)


def swap(value):
    return move(value, lambda x, z, y, c: (x, z, y, 1 - c))


def along_y(value, step):
    return move(value, lambda x, z, y, c: (x, z, y + step, c))


def along_z(value, step):
    return move(value, lambda x, z, y, c: (x, z + step, y, c))


def add(*terms):
    total = terms[0].astype(F32)
    for term in terms[1:]:
        total = total + term.astype(F32)
    return total


def ring_scatter(chunk, shift):
    far = chunk(2).astype(BF)
    half = far.shape[0] // 2
    from_left = shift(far[:half], 1)
    from_right = shift(far[half:], -1)
    right = chunk(1)
    left = chunk(-1)
    low_b = shift(right[half:].astype(BF), 1)
    up_a = shift(left[:half].astype(BF), -1)
    low_a = shift(add(right[:half], from_left).astype(BF), 1)
    up_b = shift(add(left[half:], from_right).astype(BF), -1)
    own = chunk(0)
    return jnp.concatenate([add(own[:half], up_a, low_a), add(own[half:], low_b, up_b)], axis=0)


def pair_scatter(rows, weights, width):
    y, c = lax.axis_index("y"), lax.axis_index("c")

    def term(step, core):
        start = (lax.rem(y + step + N, N) * 2 + core) * width
        columns = lax.dynamic_slice_in_dim(weights, start, width, 1)
        return jnp.dot(rows, columns, preferred_element_type=F32)

    arrived = {d: swap(term(d, 1 - c).astype(BF)) for d in (2, 1, -1, 0)}
    return lambda d: add(term(d, c), arrived[d])


def body(
    context, w_out, residual, norm_gain, w_join, dec_state, gate_s, gate_h, gate_bias, owner, pad_mask, cotangent
):
    x, z, y, c = (lax.axis_index(a) for a in AXES)
    n_owner = N * N
    tokens, width = residual.shape
    slot_rows, features = dec_state.shape
    most = slot_rows // n_owner

    onehot = (owner == jnp.arange(n_owner, dtype=jnp.int32)[None, :]).astype(BF)
    ahead = jnp.tril(jnp.ones((tokens, tokens), BF), -1)
    before = jnp.dot(ahead, onehot, preferred_element_type=F32)
    rank = jnp.sum(before * onehot.astype(F32), axis=1).astype(jnp.int32)
    slots = owner[:, 0] * most + rank
    select = (slots[:, None] == jnp.arange(slot_rows, dtype=jnp.int32)[None, :]).astype(BF)

    both = jnp.concatenate([dec_state, cotangent], axis=1).reshape(n_owner, most, 2 * features)
    both = lax.all_to_all(both, ("x", "z"), 0, 0, tiled=True).reshape(slot_rows, 2 * features)
    both = jnp.dot(select, both, preferred_element_type=F32).astype(BF)
    state_t, outer_t = both[:, :features].astype(F32), both[:, features:].astype(F32)

    summed = ring_scatter(pair_scatter(context, w_out, width), along_y)
    mixed = residual.astype(F32) + summed
    squares = jnp.sum(mixed * mixed, axis=1)
    rows = (mixed * norm_gain[None, :] * pad_mask.astype(F32)[:, None]).astype(BF)
    rows_t = lax.all_gather(rows.T, "x")

    total = squares.reshape(2, -1)
    total = total + swap(total)
    total = total + move(total, lambda x, z, y, c: (x, z, y ^ 1, c))
    total = total + move(total, lambda x, z, y, c: (x, z, y ^ 2, c))
    scale = lax.rsqrt(total.reshape(-1) / (width * N * 2) + 1e-05)[:, None]

    part = pair_scatter(rows, w_join, features)
    sums = [along_y(part(d).astype(BF), d) for d in (2, 1, -1)]
    hidden = (add(part(0), *sums) * scale).astype(BF)

    def gates(state, hidden):
        gate = jax.nn.sigmoid(gate_s[None, :] * state + gate_h[None, :] * hidden + gate_bias[None, :])
        return gate, gate * (1.0 - gate) * hidden

    gate, slope = gates(state_t, hidden.astype(F32))
    grad = (outer_t * (gate + slope * gate_h[None, :]) * scale).astype(BF)

    grad = move(grad, lambda x, z, y, c: (y, z, x, c))
    pieces = [grad] + [along_y(grad, -d) for d in (1, 2, 3)]
    pieces = [(piece, swap(piece)) for piece in pieces]
    stacked = jnp.stack(
        [jnp.concatenate([jnp.where(c == 0, a, b), jnp.where(c == 0, b, a)], axis=1) for a, b in pieces]
    )
    order = lax.rem(y + jnp.arange(N), N)
    rows_y = jnp.take(rows_t, order, axis=0)

    def grad_term(step):
        start = lax.rem(z + step + N, N) * (2 * features // N)
        columns = lax.dynamic_slice_in_dim(stacked, start, 2 * features // N, 2)
        return lax.dot_general(rows_y, columns, (((0, 2), (0, 1)), ((), ())), preferred_element_type=F32)

    join_grad = ring_scatter(grad_term, along_z)

    placed = lax.dot_general(select, hidden, (((0,), (0,)), ((), ())), preferred_element_type=F32)
    placed = placed.astype(BF).reshape(n_owner, most, features)
    placed = lax.all_to_all(placed, ("x", "z"), 0, 0, tiled=True).reshape(slot_rows, features).astype(F32)
    state = dec_state.astype(F32)
    gate, slope = gates(state, placed)
    joined = (state + gate * placed).astype(BF)
    state_grad = (cotangent.astype(F32) * (1.0 + slope * gate_s[None, :])).astype(BF)
    return joined, state_grad, join_grad


def solution(mesh):
    fine = Mesh(mesh.devices.reshape(N, N, N, 2), AXES)
    dp, mp = ("x", "z"), ("y", "c")
    in_specs = (
        P(dp, mp),
        P(mp, None),
        P(dp, mp),
        P(mp),
        P(mp, None),
        P(dp, mp),
        P(mp),
        P(mp),
        P(mp),
        P(dp, None),
        P(dp),
        P(dp, mp),
    )
    out_specs = (P(dp, mp), P(dp, mp), P(mp, dp))
    return jax.shard_map(body, mesh=fine, in_specs=in_specs, out_specs=out_specs, check_vma=False)
```

```python
import functools

import jax
import jax.numpy as jnp
from jax import lax
from jax.experimental import pallas as pl
from jax.experimental.pallas import tpu as pltpu
from jax.sharding import Mesh, PartitionSpec as P

AXES = ("x", "z", "y", "c")
N = 4
BF = jnp.bfloat16
F32 = jnp.float32


def move(value, where):
    pairs = []
    for x in range(N):
        for z in range(N):
            for y in range(N):
                for c in range(2):
                    tx, tz, ty, tc = where(x, z, y, c)
                    pairs.append(
                        (
                            ((x * N + z) * N + y) * 2 + c,
                            (((tx % N) * N + tz % N) * N + ty % N) * 2 + tc % 2,
                        )
                    )
    return lax.ppermute(value, AXES, pairs)


def swap(value):
    return move(value, lambda x, z, y, c: (x, z, y, 1 - c))


def along_y(value, step):
    return move(value, lambda x, z, y, c: (x, z, y + step, c))


def along_x(value, step):
    return move(value, lambda x, z, y, c: (x + step, z, y, c))


def add(*terms):
    total = terms[0].astype(F32)
    for term in terms[1:]:
        total = total + term.astype(F32)
    return total


def after(value, *others):
    return lax.optimization_barrier((value, *others))[0]


def product_kernel(n, width, n_in, emit, starts, rows, weights, *refs):
    extra, outs = refs[:n_in], refs[n_in:-2]
    blocks, arrived = refs[-2:]
    copies = []
    for i in range(n):
        columns = pl.ds(pl.multiple_of(starts[i], width), width)
        copies.append(pltpu.make_async_copy(weights.at[:, columns], blocks.at[i], arrived.at[i]))
        copies[i].start()
    for i in range(n):
        copies[i].wait()
        emit(i, jnp.dot(rows[...], blocks[i], preferred_element_type=F32), starts, extra, outs)


def products(rows, weights, starts, n, width, emit, out_shapes, extra=()):
    depth = rows.shape[1]
    whole = pl.BlockSpec(memory_space=pltpu.VMEM)
    return pl.pallas_call(
        functools.partial(product_kernel, n, width, len(extra), emit),
        out_shape=out_shapes,
        in_specs=[pl.BlockSpec(memory_space=pltpu.SMEM), whole, pl.BlockSpec(memory_space=pltpu.HBM)] + [whole] * len(extra),
        out_specs=[whole] * len(out_shapes),
        scratch_shapes=[pltpu.VMEM((n, depth, width), BF), pltpu.SemaphoreType.DMA((n,))],
        compiler_params=pltpu.CompilerParams(vmem_limit_bytes=40 << 20),
        cost_estimate=pl.CostEstimate(
            flops=2 * n * rows.shape[0] * depth * width, bytes_accessed=2 * n * depth * width, transcendentals=0
        ),
    )(starts, rows, weights, *extra)


def shape(rows, columns, dtype):
    return jax.ShapeDtypeStruct((rows, columns), dtype)


def project(context, w_out, width):
    y, c = lax.axis_index("y"), lax.axis_index("c")
    tokens = context.shape[0]
    half = tokens // 2

    def starts(core, *steps):
        return jnp.stack([(lax.rem(y + d + N, N) * 2 + core) * width for d in steps]).astype(jnp.int32)

    def emit_plain(i, value, starts, extra, outs):
        outs[i][...] = value.astype(BF)

    (send_2,) = products(context, w_out, starts(1 - c, 2), 1, width, emit_plain, [shape(tokens, width, BF)])
    got_2 = swap(send_2)
    sends = products(
        context, w_out, starts(1 - c, 1, -1, 0), 3, width, emit_plain, [shape(tokens, width, BF)] * 3
    )
    got_r, got_l, got_o = [swap(s) for s in sends]

    def emit_far(i, value, starts, extra, outs):
        value = value + extra[0][...].astype(F32)
        outs[0][...] = value[:half].astype(BF)
        outs[1][...] = value[half:].astype(BF)

    far_a, far_b = products(
        context, w_out, starts(c, 2), 1, width, emit_far, [shape(half, width, BF)] * 2, (got_2,)
    )
    from_left, from_right = along_y(far_a, 1), along_y(far_b, -1)

    def emit_near(i, value, starts, extra, outs):
        value = value + extra[i][...].astype(F32)
        outs[2 * i][...] = value[:half].astype(outs[2 * i].dtype)
        outs[2 * i + 1][...] = value[half:].astype(outs[2 * i + 1].dtype)

    right_a, right_b, left_a, left_b, own_a, own_b = products(
        context,
        w_out,
        starts(c, 1, -1, 0),
        3,
        width,
        emit_near,
        [shape(half, width, t) for t in (F32, BF, BF, F32, F32, F32)],
        (got_r, got_l, got_o),
    )
    low_b, up_a = along_y(right_b, 1), along_y(left_a, -1)
    low_a = along_y(add(right_a, from_left).astype(BF), 1)
    up_b = along_y(add(left_b, from_right).astype(BF), -1)
    return add(own_a, up_a, low_a), add(own_b, low_b, up_b), (low_b, up_a)


def join(rows, w_join, width):
    y, c = lax.axis_index("y"), lax.axis_index("c")
    half = rows.shape[0] // 2

    def emit(i, value, starts, extra, outs):
        first, second = value[:half], value[half:]
        mine = starts[2] == 0
        outs[2 * i][...] = jnp.where(mine, second, first).astype(BF)
        outs[2 * i + 1][...] = jnp.where(mine, first, second)

    def pair(*steps):
        starts = jnp.stack([lax.rem(y + d + N, N) * width for d in steps] + [c]).astype(jnp.int32)
        shapes = [shape(half, width, BF), shape(half, width, F32)] * 2
        return products(rows, w_join, starts, 2, width, emit, shapes)

    s2, o2, s1, o1 = pair(2, 1)
    g2, g1 = swap(s2), swap(s1)
    s3, o3, s0, o0 = pair(-1, 0)
    g3, g0 = swap(s3), swap(s0)
    terms = [along_y(add(o, g).astype(BF), d) for o, g, d in ((o2, g2, 2), (o1, g1, 1), (o3, g3, -1))]
    return add(o0, g0, *terms)


def body(
    context, w_out, residual, norm_gain, w_join, dec_state, gate_s, gate_h, gate_bias, owner, pad_mask, cotangent
):
    x, z, y, c = (lax.axis_index(a) for a in AXES)
    n_owner = N * N
    tokens, width = residual.shape
    half = tokens // 2
    slot_rows, features = dec_state.shape
    most = slot_rows // n_owner

    onehot = (owner == jnp.arange(n_owner, dtype=jnp.int32)[None, :]).astype(BF)
    ahead = jnp.tril(jnp.ones((tokens, tokens), BF), -1)
    before = jnp.dot(ahead, onehot, preferred_element_type=F32)
    rank = jnp.sum(before * onehot.astype(F32), axis=1).astype(jnp.int32)
    slots = owner[:, 0] * most + rank
    select = (slots[:, None] == jnp.arange(slot_rows, dtype=jnp.int32)[None, :]).astype(BF)

    sum_a, sum_b, late = project(context, w_out, width)

    both = jnp.concatenate([dec_state, cotangent], axis=1).reshape(n_owner, most, 2 * features)
    both = lax.all_to_all(after(both, *late), ("x", "z"), 0, 0, tiled=True).reshape(slot_rows, 2 * features)
    both = jnp.dot(select, both, preferred_element_type=F32).astype(BF)
    first = c == 0
    keep = jnp.where(first, both[:half], both[half:])
    got = swap(jnp.where(first, both[half:], both[:half]))

    def widen(mine, other):
        return jnp.where(
            first, jnp.concatenate([mine, other], axis=-1), jnp.concatenate([other, mine], axis=-1)
        )

    state_t = widen(keep[:, :features], got[:, :features]).astype(F32)
    outer_t = widen(keep[:, features:], got[:, features:]).astype(F32)
    params = jnp.stack([gate_s, gate_h, gate_bias])
    params_t = widen(params, swap(params))

    gain, mask = norm_gain[None, :], pad_mask.astype(F32)[:, None]
    residual = residual.astype(F32)
    mixed = jnp.concatenate([residual[:half] + sum_a, residual[half:] + sum_b], axis=0)
    squares = jnp.sum(mixed * mixed, axis=1)
    rows = (mixed * gain * mask).astype(BF)
    rows_z = lax.all_gather(rows, "z", axis=0, tiled=True)

    total = squares.reshape(2, -1)
    total = total + swap(total)
    total = total + move(total, lambda x, z, y, c: (x, z, y ^ 1, c))
    total = total + move(total, lambda x, z, y, c: (x, z, y ^ 2, c))
    scale = lax.rsqrt(total / (width * N * 2) + 1e-05)
    scale = jnp.where(first, scale[0], scale[1])[:, None]

    hidden = (join(rows, w_join, 2 * features) * scale).astype(BF)

    def gates(params, state, hidden):
        gate = jax.nn.sigmoid(params[0][None, :] * state + params[1][None, :] * hidden + params[2][None, :])
        return gate, gate * (1.0 - gate) * hidden

    gate, slope = gates(params_t, state_t, hidden.astype(F32))
    grad = (outer_t * (gate + slope * params_t[1][None, :]) * scale).astype(BF)

    grad = grad.reshape(half, N, -1).transpose(1, 0, 2)
    grad = lax.all_to_all(grad, "z", 0, 0, tiled=True)
    pieces = [grad] + [along_y(grad, -d) for d in (1, 2, 3)]
    swapped = [swap(piece) for piece in pieces]
    grads = jnp.stack(
        [jnp.where(first, jnp.concatenate([a, b], axis=1), jnp.concatenate([b, a], axis=1)) for a, b in zip(pieces, swapped)]
    )
    grads = grads.reshape(N, N * tokens, -1)

    def grad_term(step, part):
        columns = lax.dynamic_index_in_dim(grads, lax.rem(x + step - y + 2 * N, N), 0, keepdims=False)
        rows = rows_z[:, : width // 2] if part == 0 else rows_z[:, width // 2 :]
        return lax.dot_general(rows, columns, (((0,), (0,)), ((), ())), preferred_element_type=F32)

    from_left = along_x(grad_term(2, 0).astype(BF), 1)
    from_right = along_x(grad_term(2, 1).astype(BF), -1)
    low_b = along_x(grad_term(1, 1).astype(BF), 1)
    up_a = along_x(grad_term(-1, 0).astype(BF), -1)
    low_a = along_x(add(grad_term(1, 0), from_left).astype(BF), 1)
    up_b = along_x(add(grad_term(-1, 1), from_right).astype(BF), -1)
    join_grad = jnp.concatenate(
        [add(grad_term(0, 0), up_a, low_a), add(grad_term(0, 1), low_b, up_b)], axis=0
    )

    late_hidden = after(hidden, swapped[0])
    keep = jnp.where(first, late_hidden[:, :features], late_hidden[:, features:])
    got = swap(jnp.where(first, late_hidden[:, features:], late_hidden[:, :features]))
    rows_h = jnp.where(first, jnp.concatenate([keep, got], axis=0), jnp.concatenate([got, keep], axis=0))
    placed = lax.dot_general(select, rows_h, (((0,), (0,)), ((), ())), preferred_element_type=F32)
    placed = placed.astype(BF).reshape(n_owner, most, features)
    placed = lax.all_to_all(placed, ("x", "z"), 0, 0, tiled=True).reshape(slot_rows, features).astype(F32)
    state = dec_state.astype(F32)
    gate, slope = gates(params, state, placed)
    joined = (state + gate * placed).astype(BF)
    state_grad = (cotangent.astype(F32) * (1.0 + slope * gate_s[None, :])).astype(BF)
    return joined, state_grad, join_grad


def solution(mesh):
    fine = Mesh(mesh.devices.reshape(N, N, N, 2), AXES)
    dp, mp = ("x", "z"), ("y", "c")
    in_specs = (
        P(dp, mp),
        P(mp, None),
        P(dp, mp),
        P(mp),
        P(mp, None),
        P(dp, mp),
        P(mp),
        P(mp),
        P(mp),
        P(dp, None),
        P(dp),
        P(dp, mp),
    )
    out_specs = (P(dp, mp), P(dp, mp), P(mp, dp))
    return jax.shard_map(body, mesh=fine, in_specs=in_specs, out_specs=out_specs, check_vma=False)
```

```python
import functools

import jax
import jax.numpy as jnp
from jax import lax
from jax.experimental import pallas as pl
from jax.experimental.pallas import tpu as pltpu
from jax.sharding import Mesh, PartitionSpec as P

AXES = ("x", "z", "y", "c")
N = 4
BF = jnp.bfloat16
F32 = jnp.float32


def move(value, where):
    pairs = []
    for x in range(N):
        for z in range(N):
            for y in range(N):
                for c in range(2):
                    tx, tz, ty, tc = where(x, z, y, c)
                    pairs.append(
                        (
                            ((x * N + z) * N + y) * 2 + c,
                            (((tx % N) * N + tz % N) * N + ty % N) * 2 + tc % 2,
                        )
                    )
    return lax.ppermute(value, AXES, pairs)


def swap(value):
    return move(value, lambda x, z, y, c: (x, z, y, 1 - c))


def along_y(value, step):
    return move(value, lambda x, z, y, c: (x, z, y + step, c))


def along_z(value, step):
    return move(value, lambda x, z, y, c: (x, z + step, y, c))


def along_x(value, step):
    return move(value, lambda x, z, y, c: (x + step, z, y, c))


def add(*terms):
    total = terms[0].astype(F32)
    for term in terms[1:]:
        total = total + term.astype(F32)
    return total


def after(value, *others):
    return lax.optimization_barrier((value, *others))[0]


def product_kernel(n, width, n_in, emit, starts, rows, weights, *refs):
    extra, outs = refs[:n_in], refs[n_in:-2]
    blocks, arrived = refs[-2:]
    copies = []
    for i in range(n):
        columns = pl.ds(pl.multiple_of(starts[i], width), width)
        copies.append(pltpu.make_async_copy(weights.at[:, columns], blocks.at[i], arrived.at[i]))
        copies[i].start()
    for i in range(n):
        copies[i].wait()
        emit(i, jnp.dot(rows[...], blocks[i], preferred_element_type=F32), starts, extra, outs)


def products(rows, weights, starts, n, width, emit, out_shapes, extra=()):
    depth = rows.shape[1]
    whole = pl.BlockSpec(memory_space=pltpu.VMEM)
    return pl.pallas_call(
        functools.partial(product_kernel, n, width, len(extra), emit),
        out_shape=out_shapes,
        in_specs=[pl.BlockSpec(memory_space=pltpu.SMEM), whole, pl.BlockSpec(memory_space=pltpu.HBM)] + [whole] * len(extra),
        out_specs=[whole] * len(out_shapes),
        scratch_shapes=[pltpu.VMEM((n, depth, width), BF), pltpu.SemaphoreType.DMA((n,))],
        compiler_params=pltpu.CompilerParams(vmem_limit_bytes=32 << 20),
        cost_estimate=pl.CostEstimate(
            flops=2 * n * rows.shape[0] * depth * width, bytes_accessed=2 * n * depth * width, transcendentals=0
        ),
    )(starts, rows, pltpu.with_memory_space_constraint(weights, pltpu.HBM), *extra)


def shape(rows, columns, dtype):
    return jax.ShapeDtypeStruct((rows, columns), dtype)


def project(context, w_out, width):
    y, c = lax.axis_index("y"), lax.axis_index("c")
    tokens = context.shape[0]
    half = tokens // 2
    steps = (2, 1, -1, 0)

    def emit(i, value, starts, extra, outs):
        value = value.astype(BF)
        if i < N:
            outs[i][...] = value
        else:
            outs[2 * i - N][...] = value[:half]
            outs[2 * i - N + 1][...] = value[half:]

    starts = jnp.stack(
        [(lax.rem(y + d + N, N) * 2 + core) * width for core in (1 - c, c) for d in steps]
    ).astype(jnp.int32)
    shapes = [shape(tokens, width, BF)] * N + [shape(half, width, BF)] * (2 * N)
    outs = products(context, w_out, starts, 2 * N, width, emit, shapes)
    got = [swap(out) for out in outs[:N]]
    far, right, left, own = [
        (add(outs[N + 2 * i], got[i][:half]), add(outs[N + 2 * i + 1], got[i][half:])) for i in range(N)
    ]
    from_left, from_right = along_y(far[0].astype(BF), 1), along_y(far[1].astype(BF), -1)
    right_b, left_a = right[1].astype(BF), left[0].astype(BF)
    low_b, up_a = along_y(right_b, 1), along_y(left_a, -1)
    last = add(right[0], from_left).astype(BF), add(left[1], from_right).astype(BF)
    low_a, up_b = along_y(last[0], 1), along_y(last[1], -1)
    return add(own[0], up_a, low_a), add(own[1], low_b, up_b), last


def join(rows, w_join, width):
    y, c = lax.axis_index("y"), lax.axis_index("c")
    half = rows.shape[0] // 2
    steps = (2, 1, -1, 0)

    def emit(i, value, starts, extra, outs):
        first, second = value[:half].astype(BF), value[half:].astype(BF)
        mine = starts[N] == 0
        outs[2 * i][...] = jnp.where(mine, second, first)
        outs[2 * i + 1][...] = jnp.where(mine, first, second)

    starts = jnp.stack([lax.rem(y + d + N, N) * width for d in steps] + [c]).astype(jnp.int32)
    outs = products(rows, w_join, starts, N, width, emit, [shape(half, width, BF)] * (2 * N))
    got = [swap(out) for out in outs[::2]]
    terms = [along_y(add(outs[2 * i + 1], got[i]).astype(BF), steps[i]) for i in range(N - 1)]
    return [*terms, outs[-1], got[-1]]


def body(
    context, w_out, residual, norm_gain, w_join, dec_state, gate_s, gate_h, gate_bias, owner, pad_mask, cotangent
):
    x, z, y, c = (lax.axis_index(a) for a in AXES)
    n_owner = N * N
    tokens, width = residual.shape
    half = tokens // 2
    slot_rows, features = dec_state.shape
    most = slot_rows // n_owner
    first = c == 0

    onehot = (owner == jnp.arange(n_owner, dtype=jnp.int32)[None, :]).astype(BF)
    ahead = jnp.tril(jnp.ones((tokens, tokens), BF), -1)
    before = jnp.dot(ahead, onehot, preferred_element_type=F32)
    rank = jnp.sum(before * onehot.astype(F32), axis=1).astype(jnp.int32)
    slots = owner[:, 0] * most + rank
    select = (slots[:, None] == jnp.arange(slot_rows, dtype=jnp.int32)[None, :]).astype(BF)

    both = jnp.concatenate([dec_state, cotangent], axis=1).reshape(n_owner, most, 2 * features)

    sum_a, sum_b, last = project(context, w_out, width)
    both = lax.all_to_all(after(both, *last), ("x", "z"), 0, 0, tiled=True).reshape(slot_rows, 2 * features)
    gain, mask = norm_gain[None, :], pad_mask.astype(F32)[:, None]
    residual = residual.astype(F32)
    mixed = jnp.concatenate([residual[:half] + sum_a, residual[half:] + sum_b], axis=0)
    squares = jnp.sum(mixed * mixed, axis=1)
    rows = (mixed * gain * mask).astype(BF)
    rows_z = lax.all_gather(rows, "z", axis=0, tiled=True)

    total = squares.reshape(2, -1)
    total = total + swap(total)
    total = total + move(total, lambda x, z, y, c: (x, z, y ^ 1, c))
    total = total + move(total, lambda x, z, y, c: (x, z, y ^ 2, c))
    scale = lax.rsqrt(total / (width * N * 2) + 1e-05)
    scale = jnp.where(first, scale[0], scale[1])[:, None]

    gated, both = lax.optimization_barrier((rows, both))
    terms = join(gated, w_join, 2 * features)
    both = jnp.dot(select, after(both, terms[1]), preferred_element_type=F32).astype(BF)
    keep = jnp.where(first, both[:half], both[half:])
    got = swap(jnp.where(first, both[half:], both[:half]))

    def widen(mine, other):
        return jnp.where(
            first, jnp.concatenate([mine, other], axis=-1), jnp.concatenate([other, mine], axis=-1)
        )

    state_t = widen(keep[:, :features], got[:, :features]).astype(F32)
    outer_t = widen(keep[:, features:], got[:, features:]).astype(F32)
    params = jnp.stack([gate_s, gate_h, gate_bias])
    params_t = widen(params, swap(params))

    hidden = (add(*terms) * scale).astype(BF)

    def gates(params, state, hidden):
        gate = jax.nn.sigmoid(params[0][None, :] * state + params[1][None, :] * hidden + params[2][None, :])
        return gate, gate * (1.0 - gate) * hidden

    gate, slope = gates(params_t, state_t, hidden.astype(F32))
    grad = (outer_t * (gate + slope * params_t[1][None, :]) * scale).astype(BF)

    quarter = 2 * features // N

    def quarter_for(step):
        return lax.dynamic_slice_in_dim(grad, lax.rem(z + step + N, N) * quarter, quarter, 1)

    others = {f: along_z(quarter_for(-f), -f) for f in (2, 1, 3)}
    block = jnp.stack([quarter_for(0), others[1], others[2], others[3]] * 2)
    block = lax.dynamic_slice_in_dim(block, lax.rem(N - z, N), N, 0)
    arrived = {d: along_y(block, -d) for d in (2, 1, 3)}
    pieces = [block, arrived[1], arrived[2], arrived[3]]
    swapped = [swap(piece) for piece in pieces]
    grads = jnp.stack(
        [jnp.where(first, jnp.concatenate([a, b], axis=1), jnp.concatenate([b, a], axis=1)) for a, b in zip(pieces, swapped)]
    )
    grads = grads.reshape(N, N * tokens, -1)

    def grad_term(step, part):
        columns = lax.dynamic_index_in_dim(grads, lax.rem(x + step - y + 2 * N, N), 0, keepdims=False)
        rows = rows_z[:, : width // 2] if part == 0 else rows_z[:, width // 2 :]
        return lax.dot_general(rows, columns, (((0,), (0,)), ((), ())), preferred_element_type=F32)

    from_left = along_x(grad_term(2, 0).astype(BF), 1)
    from_right = along_x(grad_term(2, 1).astype(BF), -1)
    near = grad_term(1, 1).astype(BF), grad_term(-1, 0).astype(BF)
    low_b, up_a = along_x(near[0], 1), along_x(near[1], -1)
    low_a = along_x(add(grad_term(1, 0), from_left).astype(BF), 1)
    up_b = along_x(add(grad_term(-1, 1), from_right).astype(BF), -1)
    join_grad = jnp.concatenate(
        [add(grad_term(0, 0), up_a, low_a), add(grad_term(0, 1), low_b, up_b)], axis=0
    )

    late_hidden = after(hidden, block)
    keep = jnp.where(first, late_hidden[:, :features], late_hidden[:, features:])
    got = swap(jnp.where(first, late_hidden[:, features:], late_hidden[:, :features]))
    rows_h = jnp.where(first, jnp.concatenate([keep, got], axis=0), jnp.concatenate([got, keep], axis=0))
    placed = lax.dot_general(select, rows_h, (((0,), (0,)), ((), ())), preferred_element_type=F32)
    placed = placed.astype(BF).reshape(n_owner, most, features)
    placed = lax.all_to_all(placed, ("x", "z"), 0, 0, tiled=True).reshape(slot_rows, features).astype(F32)
    state = dec_state.astype(F32)
    gate, slope = gates(params, state, placed)
    joined = (state + gate * placed).astype(BF)
    state_grad = (cotangent.astype(F32) * (1.0 + slope * gate_s[None, :])).astype(BF)
    return joined, state_grad, join_grad


def solution(mesh):
    fine = Mesh(mesh.devices.reshape(N, N, N, 2), AXES)
    dp, mp = ("x", "z"), ("y", "c")
    in_specs = (
        P(dp, mp),
        P(mp, None),
        P(dp, mp),
        P(mp),
        P(mp, None),
        P(dp, mp),
        P(mp),
        P(mp),
        P(mp),
        P(dp, None),
        P(dp),
        P(dp, mp),
    )
    out_specs = (P(dp, mp), P(dp, mp), P(mp, dp))
    return jax.shard_map(body, mesh=fine, in_specs=in_specs, out_specs=out_specs, check_vma=False)
```

```python
import functools

import jax
import jax.numpy as jnp
from jax import lax
from jax.experimental import pallas as pl
from jax.experimental.pallas import tpu as pltpu
from jax.sharding import Mesh, PartitionSpec as P

LINES = 8
AXES = ("x", "z", "y", "c")
N = 4
BF = jnp.bfloat16
F32 = jnp.float32


def move(value, where):
    pairs = []
    for x in range(N):
        for z in range(N):
            for y in range(N):
                for c in range(2):
                    tx, tz, ty, tc = where(x, z, y, c)
                    pairs.append(
                        (
                            ((x * N + z) * N + y) * 2 + c,
                            (((tx % N) * N + tz % N) * N + ty % N) * 2 + tc % 2,
                        )
                    )
    return lax.ppermute(value, AXES, pairs)


def swap(value):
    return move(value, lambda x, z, y, c: (x, z, y, 1 - c))


def along_y(value, step):
    return move(value, lambda x, z, y, c: (x, z, y + step, c))


def along_z(value, step):
    return move(value, lambda x, z, y, c: (x, z + step, y, c))


def along_x(value, step):
    return move(value, lambda x, z, y, c: (x + step, z, y, c))


def add(*terms):
    total = terms[0].astype(F32)
    for term in terms[1:]:
        total = total + term.astype(F32)
    return total


def after(value, *others):
    return lax.optimization_barrier((value, *others))[0]


def product_kernel(n, width, n_in, emit, starts, rows, weights, *refs):
    extra, outs = refs[:n_in], refs[n_in:-2]
    blocks, arrived = refs[-2:]
    copies = []
    for i in range(n):
        columns = pl.ds(pl.multiple_of(starts[i], width), width)
        copies.append(pltpu.make_async_copy(weights.at[:, columns], blocks.at[i], arrived.at[i]))
        copies[i].start()
    for i in range(n):
        copies[i].wait()
        emit(i, jnp.dot(rows[...], blocks[i], preferred_element_type=F32), starts, extra, outs)


def products(rows, weights, starts, n, width, emit, out_shapes, extra=()):
    depth = rows.shape[1]
    whole = pl.BlockSpec(memory_space=pltpu.VMEM)
    return pl.pallas_call(
        functools.partial(product_kernel, n, width, len(extra), emit),
        out_shape=out_shapes,
        in_specs=[pl.BlockSpec(memory_space=pltpu.SMEM), whole, pl.BlockSpec(memory_space=pltpu.HBM)] + [whole] * len(extra),
        out_specs=[whole] * len(out_shapes),
        scratch_shapes=[pltpu.VMEM((n, depth, width), BF), pltpu.SemaphoreType.DMA((n,))],
        compiler_params=pltpu.CompilerParams(vmem_limit_bytes=32 << 20),
        cost_estimate=pl.CostEstimate(
            flops=2 * n * rows.shape[0] * depth * width, bytes_accessed=2 * n * depth * width, transcendentals=0
        ),
    )(starts, rows, pltpu.with_memory_space_constraint(weights, pltpu.HBM), *extra)


def shape(rows, columns, dtype):
    return jax.ShapeDtypeStruct((rows, columns), dtype)


def project(context, w_out, width, exchange):
    y, c = lax.axis_index("y"), lax.axis_index("c")
    steps = (2, 1, -1, 0)

    def emit(i, value, starts, extra, outs):
        outs[i][...] = value.astype(BF)

    starts = jnp.stack(
        [(lax.rem(y + d + N, N) * 2 + core) * width for core in (1 - c, c) for d in steps]
    ).astype(jnp.int32)
    outs = products(context, w_out, starts, 2 * N, width, emit, [shape(context.shape[0], width, BF)] * (2 * N))
    got = [swap(out) for out in outs[:N]]
    sums = [add(outs[N + i], got[i]) for i in range(N)]
    sends = [value.astype(BF) for value in sums[:-1]]
    terms = [along_y(value, d) for value, d in zip(sends, steps)]
    return add(sums[-1], *terms), exchange(*sends)


def join(rows, w_join, width, squares):
    y = lax.axis_index("y")
    half = rows.shape[0] // 2
    steps = (2, 1, -1, 0)

    def emit(i, value, starts, extra, outs):
        outs[2 * i][...] = value[half:].astype(BF)
        outs[2 * i + 1][...] = value[:half].astype(BF)

    starts = jnp.stack([lax.rem(y + d + N, N) * width for d in steps]).astype(jnp.int32)
    outs = products(rows, w_join, starts, N, width, emit, [shape(half, width, BF)] * (2 * N))
    got = [swap(out) for out in outs[::2]]
    squares = squares[0] + swap(after(squares[1], outs[-1]))
    high = lax.reduce_precision(squares, 8, 7)
    middle = lax.reduce_precision(squares - high, 8, 7)
    lines = jnp.stack([high, middle, squares - high - middle])
    lines = jnp.pad(lines, ((0, LINES - 3), (0, width - half))).astype(BF)
    sends = [jnp.concatenate([add(outs[2 * i + 1], got[i]).astype(BF), lines], axis=0) for i in range(N - 1)]
    terms = [along_y(sends[i], steps[i]) for i in range(N - 1)]
    total = squares + sum(jnp.sum(term[half : half + 3, :half].astype(F32), axis=0) for term in terms)
    return [outs[-1], got[-1], *[term[:half] for term in terms]], total, sends


def body(
    context, w_out, residual, norm_gain, w_join, dec_state, gate_s, gate_h, gate_bias, owner, pad_mask, cotangent
):
    x, z, y, c = (lax.axis_index(a) for a in AXES)
    n_owner = N * N
    tokens, width = residual.shape
    half = tokens // 2
    slot_rows, features = dec_state.shape
    most = slot_rows // n_owner
    first = c == 0

    onehot = (owner == jnp.arange(n_owner, dtype=jnp.int32)[None, :]).astype(BF)
    ahead = jnp.tril(jnp.ones((tokens, tokens), BF), -1)
    before = jnp.dot(ahead, onehot, preferred_element_type=F32)
    rank = jnp.sum(before * onehot.astype(F32), axis=1).astype(jnp.int32)
    slots = owner[:, 0] * most + rank
    select = (slots[:, None] == jnp.arange(slot_rows, dtype=jnp.int32)[None, :]).astype(BF)

    both = jnp.concatenate([dec_state, cotangent], axis=1).reshape(n_owner, most, 2 * features)

    summed, both = project(
        context, w_out, width, lambda *others: lax.all_to_all(after(both, *others), ("x", "z"), 0, 0, tiled=True)
    )
    both = both.reshape(slot_rows, 2 * features)
    gain, mask = norm_gain[None, :], pad_mask.astype(F32)[:, None]
    residual = residual.astype(F32)
    mixed = residual + summed
    squares = jnp.sum(mixed * mixed, axis=1)
    rows = (mixed * gain * mask).astype(BF)
    rows = jnp.where(first, rows, jnp.concatenate([rows[half:], rows[:half]], axis=0))

    gated, both = lax.optimization_barrier((rows, both))
    squares = squares.reshape(2, half)
    squares = jnp.where(first, squares[0], squares[1]), jnp.where(first, squares[1], squares[0])
    terms, total, sends = join(gated, w_join, 2 * features, squares)
    *terms, rows_1, rows_3 = lax.optimization_barrier((*terms, along_z(rows, -1), along_z(rows, 1)))
    hidden = add(*terms)
    scale = lax.rsqrt(total / (width * N * 2) + 1e-05)[:, None]
    both = jnp.dot(select, after(both, *sends), preferred_element_type=F32).astype(BF)
    keep = jnp.where(first, both[:half], both[half:])
    got = swap(jnp.where(first, both[half:], both[:half]))

    def widen(mine, other):
        return jnp.where(
            first, jnp.concatenate([mine, other], axis=-1), jnp.concatenate([other, mine], axis=-1)
        )

    state_t = widen(keep[:, :features], got[:, :features]).astype(F32)
    outer_t = widen(keep[:, features:], got[:, features:]).astype(F32)
    params = jnp.stack([gate_s, gate_h, gate_bias])
    params_t = widen(params, swap(params))

    hidden = (hidden * scale).astype(BF)

    def gates(params, state, hidden):
        gate = jax.nn.sigmoid(params[0][None, :] * state + params[1][None, :] * hidden + params[2][None, :])
        return gate, gate * (1.0 - gate) * hidden

    gate, slope = gates(params_t, state_t, hidden.astype(F32))
    grad = (outer_t * (gate + slope * params_t[1][None, :]) * scale).astype(BF)

    quarter = 2 * features // N

    def quarter_for(step):
        return lax.dynamic_slice_in_dim(grad, lax.rem(z + step + N, N) * quarter, quarter, 1)

    others = {f: along_z(quarter_for(-f), -f) for f in (2, 1, 3)}
    block = jnp.stack([quarter_for(0), others[1], others[2], others[3]])
    rows_2 = along_z(after(rows, block), 2)
    arrived = {d: along_y(block, -d) for d in (2, 1, 3)}
    arrived[2], rows_2 = lax.optimization_barrier((arrived[2], rows_2))
    pieces = [block, arrived[1], arrived[2], arrived[3]]
    swapped = [swap(piece) for piece in pieces]
    grads = jnp.stack([jnp.stack(pair, axis=1) for pair in zip(pieces, swapped)]).reshape(N, N * tokens, quarter)
    rows_z = lax.optimization_barrier(jnp.concatenate([rows, rows_1, rows_2, rows_3], axis=0))

    def grad_term(step):
        columns = lax.dynamic_index_in_dim(grads, lax.rem(x + step - y + 2 * N, N), 0, keepdims=False)
        return lax.dot_general(rows_z, columns, (((0,), (0,)), ((), ())), preferred_element_type=F32)

    sends = [grad_term(d).astype(BF) for d in (2, 1, -1)]
    sums = [along_x(value, d) for value, d in zip(sends, (2, 1, -1))]

    late_hidden = after(hidden, block)
    keep = jnp.where(first, late_hidden[:, :features], late_hidden[:, features:])
    got = swap(jnp.where(first, late_hidden[:, features:], late_hidden[:, :features]))
    rows_h = jnp.where(first, jnp.concatenate([keep, got], axis=0), jnp.concatenate([got, keep], axis=0))
    placed = lax.dot_general(select, rows_h, (((0,), (0,)), ((), ())), preferred_element_type=F32)
    placed = placed.astype(BF).reshape(n_owner, most, features)
    placed = lax.all_to_all(placed, ("x", "z"), 0, 0, tiled=True)
    placed = placed.reshape(slot_rows, features).astype(F32)
    state = dec_state.astype(F32)
    gate, slope = gates(params, state, placed)
    joined = (state + gate * placed).astype(BF)
    state_grad = (cotangent.astype(F32) * (1.0 + slope * gate_s[None, :])).astype(BF)
    join_grad = add(grad_term(0), *sums)
    return joined, state_grad, join_grad


def solution(mesh):
    fine = Mesh(mesh.devices.reshape(N, N, N, 2), AXES)
    dp, mp = ("x", "z"), ("y", "c")
    in_specs = (
        P(dp, mp),
        P(mp, None),
        P(dp, mp),
        P(mp),
        P(mp, None),
        P(dp, mp),
        P(mp),
        P(mp),
        P(mp),
        P(dp, None),
        P(dp),
        P(dp, mp),
    )
    out_specs = (P(dp, mp), P(dp, mp), P(mp, dp))
    return jax.shard_map(body, mesh=fine, in_specs=in_specs, out_specs=out_specs, check_vma=False)
```

```python
import functools

import jax
import jax.numpy as jnp
from jax import lax
from jax.experimental import pallas as pl
from jax.experimental.pallas import tpu as pltpu
from jax.sharding import Mesh, PartitionSpec as P

LINES = 8
AXES = ("x", "z", "y", "c")
N = 4
BF = jnp.bfloat16
F32 = jnp.float32


def move(value, where):
    pairs = []
    for x in range(N):
        for z in range(N):
            for y in range(N):
                for c in range(2):
                    tx, tz, ty, tc = where(x, z, y, c)
                    pairs.append(
                        (
                            ((x * N + z) * N + y) * 2 + c,
                            (((tx % N) * N + tz % N) * N + ty % N) * 2 + tc % 2,
                        )
                    )
    return lax.ppermute(value, AXES, pairs)


def swap(value):
    return move(value, lambda x, z, y, c: (x, z, y, 1 - c))


def along_y(value, step):
    return move(value, lambda x, z, y, c: (x, z, y + step, c))


def along_z(value, step):
    return move(value, lambda x, z, y, c: (x, z + step, y, c))


def along_x(value, step):
    return move(value, lambda x, z, y, c: (x + step, z, y, c))


def add(*terms):
    total = terms[0].astype(F32)
    for term in terms[1:]:
        total = total + term.astype(F32)
    return total


def after(value, *others):
    return lax.optimization_barrier((value, *others))[0]


def product_kernel(n, width, n_in, emit, starts, rows, weights, *refs):
    extra, outs = refs[:n_in], refs[n_in:-2]
    blocks, arrived = refs[-2:]
    copies = []
    for i in range(n):
        columns = pl.ds(pl.multiple_of(starts[i], width), width)
        copies.append(pltpu.make_async_copy(weights.at[:, columns], blocks.at[i], arrived.at[i]))
        copies[i].start()
    for i in range(n):
        copies[i].wait()
        emit(i, jnp.dot(rows[...], blocks[i], preferred_element_type=F32), starts, extra, outs)


def products(rows, weights, starts, n, width, emit, out_shapes, extra=()):
    depth = rows.shape[1]
    whole = pl.BlockSpec(memory_space=pltpu.VMEM)
    return pl.pallas_call(
        functools.partial(product_kernel, n, width, len(extra), emit),
        out_shape=out_shapes,
        in_specs=[pl.BlockSpec(memory_space=pltpu.SMEM), whole, pl.BlockSpec(memory_space=pltpu.HBM)] + [whole] * len(extra),
        out_specs=[whole] * len(out_shapes),
        scratch_shapes=[pltpu.VMEM((n, depth, width), BF), pltpu.SemaphoreType.DMA((n,))],
        compiler_params=pltpu.CompilerParams(vmem_limit_bytes=32 << 20),
        cost_estimate=pl.CostEstimate(
            flops=2 * n * rows.shape[0] * depth * width, bytes_accessed=2 * n * depth * width, transcendentals=0
        ),
    )(starts, rows, pltpu.with_memory_space_constraint(weights, pltpu.HBM), *extra)


def shape(rows, columns, dtype):
    return jax.ShapeDtypeStruct((rows, columns), dtype)


def project(context, w_out, width, exchange):
    y, c = lax.axis_index("y"), lax.axis_index("c")
    steps = (2, 1, -1, 0)

    def emit(i, value, starts, extra, outs):
        outs[i][...] = value.astype(BF)

    starts = jnp.stack(
        [(lax.rem(y + d + N, N) * 2 + core) * width for core in (1 - c, c) for d in steps]
    ).astype(jnp.int32)
    outs = products(context, w_out, starts, 2 * N, width, emit, [shape(context.shape[0], width, BF)] * (2 * N))
    got = [swap(out) for out in outs[:N]]
    sums = [add(outs[N + i], got[i]) for i in range(N)]
    sends = [value.astype(BF) for value in sums[:-1]]
    terms = [along_y(value, d) for value, d in zip(sends, steps)]
    return add(sums[-1], *terms), exchange(*sends)


def join(rows, w_join, width, squares):
    y = lax.axis_index("y")
    half = rows.shape[0] // 2
    steps = (2, 1, -1, 0)

    def emit(i, value, starts, extra, outs):
        outs[2 * i][...] = value[half:].astype(BF)
        outs[2 * i + 1][...] = value[:half].astype(BF)

    starts = jnp.stack([lax.rem(y + d + N, N) * width for d in steps]).astype(jnp.int32)
    outs = products(rows, w_join, starts, N, width, emit, [shape(half, width, BF)] * (2 * N))
    got = [swap(out) for out in outs[::2]]
    squares = squares[0] + swap(after(squares[1], outs[-1]))
    high = lax.reduce_precision(squares, 8, 7)
    middle = lax.reduce_precision(squares - high, 8, 7)
    lines = jnp.stack([high, middle, squares - high - middle])
    lines = jnp.pad(lines, ((0, LINES - 3), (0, width - half))).astype(BF)
    sends = [jnp.concatenate([add(outs[2 * i + 1], got[i]).astype(BF), lines], axis=0) for i in range(N - 1)]
    own = add(outs[-1], got[-1])
    *sends, own = lax.optimization_barrier((*sends, own))
    terms = [along_y(sends[i], steps[i]) for i in range(N - 1)]
    total = squares + sum(jnp.sum(term[half : half + 3, :half].astype(F32), axis=0) for term in terms)
    return [own, *[term[:half] for term in terms]], total, sends


def body(
    context, w_out, residual, norm_gain, w_join, dec_state, gate_s, gate_h, gate_bias, owner, pad_mask, cotangent
):
    x, z, y, c = (lax.axis_index(a) for a in AXES)
    n_owner = N * N
    tokens, width = residual.shape
    half = tokens // 2
    slot_rows, features = dec_state.shape
    most = slot_rows // n_owner
    first = c == 0

    onehot = (owner == jnp.arange(n_owner, dtype=jnp.int32)[None, :]).astype(BF)
    ahead = jnp.tril(jnp.ones((tokens, tokens), BF), -1)
    before = jnp.dot(ahead, onehot, preferred_element_type=F32)
    rank = jnp.sum(before * onehot.astype(F32), axis=1).astype(jnp.int32)
    slots = owner[:, 0] * most + rank
    select = (slots[:, None] == jnp.arange(slot_rows, dtype=jnp.int32)[None, :]).astype(BF)

    both = jnp.concatenate([dec_state, cotangent], axis=1).reshape(n_owner, most, 2 * features)

    summed, both = project(
        context, w_out, width, lambda *others: lax.all_to_all(after(both, *others), ("x", "z"), 0, 0, tiled=True)
    )
    both = both.reshape(slot_rows, 2 * features)
    gain, mask = norm_gain[None, :], pad_mask.astype(F32)[:, None]
    residual = residual.astype(F32)
    mixed = residual + summed
    squares = jnp.sum(mixed * mixed, axis=1)
    rows = (mixed * gain * mask).astype(BF)
    rows = jnp.where(first, rows, jnp.concatenate([rows[half:], rows[:half]], axis=0))

    gated, both = lax.optimization_barrier((rows, both))
    squares = squares.reshape(2, half)
    squares = jnp.where(first, squares[0], squares[1]), jnp.where(first, squares[1], squares[0])
    terms, total, sends = join(gated, w_join, 2 * features, squares)
    rows_sent = after(rows, *sends)
    rows_1, rows_3 = along_z(rows_sent, -1), along_z(rows_sent, 1)
    hidden = add(*terms)
    scale = lax.rsqrt(total / (width * N * 2) + 1e-05)[:, None]
    both = jnp.dot(select, after(both, *sends), preferred_element_type=F32).astype(BF)
    keep = jnp.where(first, both[:half], both[half:])
    got = swap(jnp.where(first, both[half:], both[:half]))

    def widen(mine, other):
        return jnp.where(
            first, jnp.concatenate([mine, other], axis=-1), jnp.concatenate([other, mine], axis=-1)
        )

    state_t = widen(keep[:, :features], got[:, :features]).astype(F32)
    outer_t = widen(keep[:, features:], got[:, features:]).astype(F32)
    params = jnp.stack([gate_s, gate_h, gate_bias])
    params_t = widen(params, swap(params))

    hidden = (hidden * scale).astype(BF)

    def gates(params, state, hidden):
        gate = jax.nn.sigmoid(params[0][None, :] * state + params[1][None, :] * hidden + params[2][None, :])
        return gate, gate * (1.0 - gate) * hidden

    gate, slope = gates(params_t, state_t, hidden.astype(F32))
    grad = (outer_t * (gate + slope * params_t[1][None, :]) * scale).astype(BF)

    quarter = 2 * features // N

    def quarter_for(step):
        return lax.dynamic_slice_in_dim(grad, lax.rem(z + step + N, N) * quarter, quarter, 1)

    others = {f: along_z(quarter_for(-f), -f) for f in (2, 1, 3)}
    block = jnp.stack([quarter_for(0), others[1], others[2], others[3]])
    block, rows_1, rows_3 = lax.optimization_barrier((block, rows_1, rows_3))
    rows_2 = along_z(after(rows, block), 2)
    arrived = {d: along_y(block, -d) for d in (2, 1, 3)}
    arrived[1], arrived[2], arrived[3], rows_2 = lax.optimization_barrier((arrived[1], arrived[2], arrived[3], rows_2))
    pieces = [block, arrived[1], arrived[2], arrived[3]]
    swapped = [swap(piece) for piece in pieces]
    grads = jnp.stack([jnp.stack(pair, axis=1) for pair in zip(pieces, swapped)]).reshape(N, N * tokens, quarter)
    rows_z = lax.optimization_barrier(jnp.concatenate([rows, rows_1, rows_2, rows_3], axis=0))

    keep = jnp.where(first, hidden[:, :features], hidden[:, features:])
    got = swap(jnp.where(first, hidden[:, features:], hidden[:, :features]))
    rows_h = jnp.where(first, jnp.concatenate([keep, got], axis=0), jnp.concatenate([got, keep], axis=0))
    placed = lax.dot_general(select, rows_h, (((0,), (0,)), ((), ())), preferred_element_type=F32)
    placed = after(placed.astype(BF), block).reshape(n_owner, most, features)
    placed = lax.all_to_all(placed, ("x", "z"), 0, 0, tiled=True)
    placed = placed.reshape(slot_rows, features).astype(F32)

    def grad_term(step, part):
        columns = lax.dynamic_index_in_dim(grads, lax.rem(x + step - y + 2 * N, N), 0, keepdims=False)
        lines = rows_z[:, : width // 2] if part == 0 else rows_z[:, width // 2 :]
        return lax.dot_general(lines, columns, (((0,), (0,)), ((), ())), preferred_element_type=F32)

    from_left = along_x(grad_term(2, 0).astype(BF), 1)
    from_right = along_x(grad_term(2, 1).astype(BF), -1)
    near = grad_term(1, 1).astype(BF), grad_term(-1, 0).astype(BF)
    low_b, up_a = along_x(near[0], 1), along_x(near[1], -1)
    last = add(grad_term(1, 0), from_left).astype(BF), add(grad_term(-1, 1), from_right).astype(BF)
    low_a, up_b = along_x(last[0], 1), along_x(last[1], -1)
    placed = placed + from_left[0, 0] * 0.0
    state = dec_state.astype(F32)
    gate, slope = gates(params, state, placed)
    joined = (state + gate * placed).astype(BF)
    state_grad = (cotangent.astype(F32) * (1.0 + slope * gate_s[None, :])).astype(BF)
    join_grad = jnp.concatenate(
        [add(grad_term(0, 0), up_a, low_a), add(grad_term(0, 1), low_b, up_b)], axis=0
    )
    return joined, state_grad, join_grad


def solution(mesh):
    fine = Mesh(mesh.devices.reshape(N, N, N, 2), AXES)
    dp, mp = ("x", "z"), ("y", "c")
    in_specs = (
        P(dp, mp),
        P(mp, None),
        P(dp, mp),
        P(mp),
        P(mp, None),
        P(dp, mp),
        P(mp),
        P(mp),
        P(mp),
        P(dp, None),
        P(dp),
        P(dp, mp),
    )
    out_specs = (P(dp, mp), P(dp, mp), P(mp, dp))
    return jax.shard_map(body, mesh=fine, in_specs=in_specs, out_specs=out_specs, check_vma=False)
```

```python
import functools

import jax
import jax.numpy as jnp
from jax import lax
from jax.experimental import pallas as pl
from jax.experimental.pallas import tpu as pltpu
from jax.sharding import Mesh, PartitionSpec as P

LINES = 8
AXES = ("x", "z", "y", "c")
N = 4
BF = jnp.bfloat16
F32 = jnp.float32


def move(value, where):
    pairs = []
    for x in range(N):
        for z in range(N):
            for y in range(N):
                for c in range(2):
                    tx, tz, ty, tc = where(x, z, y, c)
                    pairs.append(
                        (
                            ((x * N + z) * N + y) * 2 + c,
                            (((tx % N) * N + tz % N) * N + ty % N) * 2 + tc % 2,
                        )
                    )
    return lax.ppermute(value, AXES, pairs)


def swap(value):
    return move(value, lambda x, z, y, c: (x, z, y, 1 - c))


def along_y(value, step):
    return move(value, lambda x, z, y, c: (x, z, y + step, c))


def along_z(value, step):
    return move(value, lambda x, z, y, c: (x, z + step, y, c))


def along_x(value, step):
    return move(value, lambda x, z, y, c: (x + step, z, y, c))


def add(*terms):
    total = terms[0].astype(F32)
    for term in terms[1:]:
        total = total + term.astype(F32)
    return total


def after(value, *others):
    return lax.optimization_barrier((value, *others))[0]


def product_kernel(n, width, n_in, emit, starts, rows, weights, *refs):
    extra, outs = refs[:n_in], refs[n_in:-2]
    blocks, arrived = refs[-2:]
    copies = []
    for i in range(n):
        columns = pl.ds(pl.multiple_of(starts[i], width), width)
        copies.append(pltpu.make_async_copy(weights.at[:, columns], blocks.at[i], arrived.at[i]))
        copies[i].start()
    for i in range(n):
        copies[i].wait()
        emit(i, jnp.dot(rows[...], blocks[i], preferred_element_type=F32), starts, extra, outs)


def products(rows, weights, starts, n, width, emit, out_shapes, extra=()):
    depth = rows.shape[1]
    whole = pl.BlockSpec(memory_space=pltpu.VMEM)
    return pl.pallas_call(
        functools.partial(product_kernel, n, width, len(extra), emit),
        out_shape=out_shapes,
        in_specs=[pl.BlockSpec(memory_space=pltpu.SMEM), whole, pl.BlockSpec(memory_space=pltpu.HBM)] + [whole] * len(extra),
        out_specs=[whole] * len(out_shapes),
        scratch_shapes=[pltpu.VMEM((n, depth, width), BF), pltpu.SemaphoreType.DMA((n,))],
        compiler_params=pltpu.CompilerParams(vmem_limit_bytes=32 << 20),
        cost_estimate=pl.CostEstimate(
            flops=2 * n * rows.shape[0] * depth * width, bytes_accessed=2 * n * depth * width, transcendentals=0
        ),
    )(starts, rows, pltpu.with_memory_space_constraint(weights, pltpu.HBM), *extra)


def shape(rows, columns, dtype):
    return jax.ShapeDtypeStruct((rows, columns), dtype)


def project(context, w_out, width, exchange):
    y, c = lax.axis_index("y"), lax.axis_index("c")
    steps = (-1, 1, 2, 0)

    def emit(i, value, starts, extra, outs):
        outs[i][...] = value.astype(BF)

    starts = jnp.stack(
        [(lax.rem(y + d + N, N) * 2 + core) * width for core in (1 - c, c) for d in steps]
    ).astype(jnp.int32)
    outs = products(context, w_out, starts, 2 * N, width, emit, [shape(context.shape[0], width, BF)] * (2 * N))
    got = [swap(out) for out in outs[:N]]
    sums = [add(outs[N + i], got[i]) for i in range(N)]
    sends = [value.astype(BF) for value in sums[:-1]]
    terms = [along_y(value, d) for value, d in zip(sends, steps)]
    return add(sums[-1], *terms), exchange(*sends)


def join(rows, w_join, width, squares):
    y = lax.axis_index("y")
    half = rows.shape[0] // 2
    steps = (2, 1, -1, 0)

    def emit(i, value, starts, extra, outs):
        outs[2 * i][...] = value[half:].astype(BF)
        outs[2 * i + 1][...] = value[:half].astype(BF)

    starts = jnp.stack([lax.rem(y + d + N, N) * width for d in steps]).astype(jnp.int32)
    outs = products(rows, w_join, starts, N, width, emit, [shape(half, width, BF)] * (2 * N))
    got = [swap(out) for out in outs[::2]]
    squares = squares[0] + swap(after(squares[1], outs[-1]))
    high = lax.reduce_precision(squares, 8, 7)
    middle = lax.reduce_precision(squares - high, 8, 7)
    lines = jnp.stack([high, middle, squares - high - middle])
    lines = jnp.pad(lines, ((0, LINES - 3), (0, width - half))).astype(BF)
    sends = [jnp.concatenate([add(outs[2 * i + 1], got[i]).astype(BF), lines], axis=0) for i in range(N - 1)]
    own = add(outs[-1], got[-1])
    *sends, own = lax.optimization_barrier((*sends, own))
    terms = [along_y(sends[i], steps[i]) for i in range(N - 1)]
    total = squares + sum(jnp.sum(term[half : half + 3, :half].astype(F32), axis=0) for term in terms)
    return [own, *[term[:half] for term in terms]], total, sends


def body(
    context, w_out, residual, norm_gain, w_join, dec_state, gate_s, gate_h, gate_bias, owner, pad_mask, cotangent
):
    x, z, y, c = (lax.axis_index(a) for a in AXES)
    n_owner = N * N
    tokens, width = residual.shape
    half = tokens // 2
    slot_rows, features = dec_state.shape
    most = slot_rows // n_owner
    first = c == 0

    onehot = (owner == jnp.arange(n_owner, dtype=jnp.int32)[None, :]).astype(BF)
    ahead = jnp.tril(jnp.ones((tokens, tokens), BF), -1)
    before = jnp.dot(ahead, onehot, preferred_element_type=F32)
    rank = jnp.sum(before * onehot.astype(F32), axis=1).astype(jnp.int32)
    slots = owner[:, 0] * most + rank
    select = (slots[:, None] == jnp.arange(slot_rows, dtype=jnp.int32)[None, :]).astype(BF)

    both = jnp.concatenate([dec_state, cotangent], axis=1).reshape(n_owner, most, 2 * features)

    summed, both = project(
        context, w_out, width, lambda *others: lax.all_to_all(after(both, *others), ("x", "z"), 0, 0, tiled=True)
    )
    both = both.reshape(slot_rows, 2 * features)
    gain, mask = norm_gain[None, :], pad_mask.astype(F32)[:, None]
    residual = residual.astype(F32)
    mixed = residual + summed
    squares = jnp.sum(mixed * mixed, axis=1)
    rows = (mixed * gain * mask).astype(BF)
    rows = jnp.where(first, rows, jnp.concatenate([rows[half:], rows[:half]], axis=0))

    gated, both = lax.optimization_barrier((rows, both))
    squares = squares.reshape(2, half)
    squares = jnp.where(first, squares[0], squares[1]), jnp.where(first, squares[1], squares[0])
    terms, total, sends = join(gated, w_join, 2 * features, squares)
    rows_sent = after(rows, *sends)
    rows_1, rows_3 = along_z(rows_sent, -1), along_z(rows_sent, 1)
    hidden = add(*terms)
    scale = lax.rsqrt(total / (width * N * 2) + 1e-05)[:, None]
    both = jnp.dot(select, after(both, *sends), preferred_element_type=F32).astype(BF)
    keep = jnp.where(first, both[:half], both[half:])
    got = swap(jnp.where(first, both[half:], both[:half]))

    def widen(mine, other):
        return jnp.where(
            first, jnp.concatenate([mine, other], axis=-1), jnp.concatenate([other, mine], axis=-1)
        )

    state_t = widen(keep[:, :features], got[:, :features]).astype(F32)
    outer_t = widen(keep[:, features:], got[:, features:]).astype(F32)
    params = jnp.stack([gate_s, gate_h, gate_bias])
    params_t = widen(params, swap(params))

    hidden = (hidden * scale).astype(BF)

    def gates(params, state, hidden):
        gate = jax.nn.sigmoid(params[0][None, :] * state + params[1][None, :] * hidden + params[2][None, :])
        return gate, gate * (1.0 - gate) * hidden

    gate, slope = gates(params_t, state_t, hidden.astype(F32))
    grad = (outer_t * (gate + slope * params_t[1][None, :]) * scale).astype(BF)

    quarter = 2 * features // N

    def quarter_for(step):
        return lax.dynamic_slice_in_dim(grad, lax.rem(z + step + N, N) * quarter, quarter, 1)

    others = {f: along_z(quarter_for(-f), -f) for f in (2, 1, 3)}
    block = jnp.stack([quarter_for(0), others[1], others[2], others[3]])
    block, rows_1, rows_3 = lax.optimization_barrier((block, rows_1, rows_3))
    rows_2 = along_z(after(rows, block), 2)
    arrived = {d: along_y(block, -d) for d in (2, 1, 3)}
    arrived[1], arrived[2], arrived[3], rows_2 = lax.optimization_barrier((arrived[1], arrived[2], arrived[3], rows_2))
    pieces = [block, arrived[1], arrived[2], arrived[3]]
    swapped = [swap(piece) for piece in pieces]
    grads = jnp.stack([jnp.stack(pair, axis=1) for pair in zip(pieces, swapped)]).reshape(N, N * tokens, quarter)
    rows_z = lax.optimization_barrier(jnp.concatenate([rows, rows_1, rows_2, rows_3], axis=0))

    keep = jnp.where(first, hidden[:, :features], hidden[:, features:])
    got = swap(jnp.where(first, hidden[:, features:], hidden[:, :features]))
    rows_h = jnp.where(first, jnp.concatenate([keep, got], axis=0), jnp.concatenate([got, keep], axis=0))
    placed = lax.dot_general(select, rows_h, (((0,), (0,)), ((), ())), preferred_element_type=F32)
    placed = after(placed.astype(BF), block).reshape(n_owner, most, features)
    placed = lax.all_to_all(placed, ("x", "z"), 0, 0, tiled=True)
    placed = placed.reshape(slot_rows, features).astype(F32)

    def grad_term(step, part):
        columns = lax.dynamic_index_in_dim(grads, lax.rem(x + step - y + 2 * N, N), 0, keepdims=False)
        lines = rows_z[:, : width // 2] if part == 0 else rows_z[:, width // 2 :]
        return lax.dot_general(lines, columns, (((0,), (0,)), ((), ())), preferred_element_type=F32)

    from_left = along_x(grad_term(2, 0).astype(BF), 1)
    from_right = along_x(grad_term(2, 1).astype(BF), -1)
    near = grad_term(1, 1).astype(BF), grad_term(-1, 0).astype(BF)
    low_b, up_a = along_x(near[0], 1), along_x(near[1], -1)
    last = add(grad_term(1, 0), from_left).astype(BF), add(grad_term(-1, 1), from_right).astype(BF)
    low_a, up_b = along_x(last[0], 1), along_x(last[1], -1)
    placed = placed + from_left[0, 0] * 0.0
    state = dec_state.astype(F32)
    gate, slope = gates(params, state, placed)
    joined = (state + gate * placed).astype(BF)
    state_grad = (cotangent.astype(F32) * (1.0 + slope * gate_s[None, :])).astype(BF)
    join_grad = jnp.concatenate(
        [add(grad_term(0, 0), up_a, low_a), add(grad_term(0, 1), low_b, up_b)], axis=0
    )
    return joined, state_grad, join_grad


def solution(mesh):
    fine = Mesh(mesh.devices.reshape(N, N, N, 2), AXES)
    dp, mp = ("x", "z"), ("y", "c")
    in_specs = (
        P(dp, mp),
        P(mp, None),
        P(dp, mp),
        P(mp),
        P(mp, None),
        P(dp, mp),
        P(mp),
        P(mp),
        P(mp),
        P(dp, None),
        P(dp),
        P(dp, mp),
    )
    out_specs = (P(dp, mp), P(dp, mp), P(mp, dp))
    return jax.shard_map(body, mesh=fine, in_specs=in_specs, out_specs=out_specs, check_vma=False)
```

```python
import functools

import jax
import jax.numpy as jnp
from jax import lax
from jax.experimental import pallas as pl
from jax.experimental.pallas import tpu as pltpu
from jax.sharding import Mesh, PartitionSpec as P

LINES = 8
AXES = ("x", "z", "y", "c")
N = 4
BF = jnp.bfloat16
F32 = jnp.float32


def move(value, where):
    pairs = []
    for x in range(N):
        for z in range(N):
            for y in range(N):
                for c in range(2):
                    tx, tz, ty, tc = where(x, z, y, c)
                    pairs.append(
                        (
                            ((x * N + z) * N + y) * 2 + c,
                            (((tx % N) * N + tz % N) * N + ty % N) * 2 + tc % 2,
                        )
                    )
    return lax.ppermute(value, AXES, pairs)


def swap(value):
    return move(value, lambda x, z, y, c: (x, z, y, 1 - c))


def along_y(value, step):
    return move(value, lambda x, z, y, c: (x, z, y + step, c))


def along_z(value, step):
    return move(value, lambda x, z, y, c: (x, z + step, y, c))


def along_x(value, step):
    return move(value, lambda x, z, y, c: (x + step, z, y, c))


def add(*terms):
    total = terms[0].astype(F32)
    for term in terms[1:]:
        total = total + term.astype(F32)
    return total


def after(value, *others):
    return lax.optimization_barrier((value, *others))[0]


def product_kernel(n, width, n_in, emit, starts, rows, weights, *refs):
    extra, outs = refs[:n_in], refs[n_in:-2]
    blocks, arrived = refs[-2:]
    copies = []
    for i in range(n):
        columns = pl.ds(pl.multiple_of(starts[i], width), width)
        copies.append(pltpu.make_async_copy(weights.at[:, columns], blocks.at[i], arrived.at[i]))
        copies[i].start()
    for i in range(n):
        copies[i].wait()
        emit(i, jnp.dot(rows[...], blocks[i], preferred_element_type=F32), starts, extra, outs)


def products(rows, weights, starts, n, width, emit, out_shapes, extra=()):
    depth = rows.shape[1]
    whole = pl.BlockSpec(memory_space=pltpu.VMEM)
    return pl.pallas_call(
        functools.partial(product_kernel, n, width, len(extra), emit),
        out_shape=out_shapes,
        in_specs=[pl.BlockSpec(memory_space=pltpu.SMEM), whole, pl.BlockSpec(memory_space=pltpu.HBM)] + [whole] * len(extra),
        out_specs=[whole] * len(out_shapes),
        scratch_shapes=[pltpu.VMEM((n, depth, width), BF), pltpu.SemaphoreType.DMA((n,))],
        compiler_params=pltpu.CompilerParams(vmem_limit_bytes=32 << 20),
        cost_estimate=pl.CostEstimate(
            flops=2 * n * rows.shape[0] * depth * width, bytes_accessed=2 * n * depth * width, transcendentals=0
        ),
    )(starts, rows, pltpu.with_memory_space_constraint(weights, pltpu.HBM), *extra)


def shape(rows, columns, dtype):
    return jax.ShapeDtypeStruct((rows, columns), dtype)


def project(context, w_out, width, exchange):
    y, c = lax.axis_index("y"), lax.axis_index("c")
    steps = (-1, 1, 2, 0)

    def emit(i, value, starts, extra, outs):
        outs[i][...] = value.astype(BF)

    starts = jnp.stack(
        [(lax.rem(y + d + N, N) * 2 + core) * width for core in (1 - c, c) for d in steps]
    ).astype(jnp.int32)
    outs = products(context, w_out, starts, 2 * N, width, emit, [shape(context.shape[0], width, BF)] * (2 * N))
    got = [swap(out) for out in outs[:N]]
    sums = [add(outs[N + i], got[i]) for i in range(N)]
    sends = [value.astype(BF) for value in sums[:-1]]
    terms = [along_y(value, d) for value, d in zip(sends, steps)]
    return add(sums[-1], *terms), exchange(*sends)


def join(rows, w_join, width, squares):
    y = lax.axis_index("y")
    half = rows.shape[0] // 2
    steps = (1, -1, 2, 0)

    def emit(i, value, starts, extra, outs):
        outs[2 * i][...] = value[half:].astype(BF)
        outs[2 * i + 1][...] = value[:half].astype(BF)

    starts = jnp.stack([lax.rem(y + d + N, N) * width for d in steps]).astype(jnp.int32)
    outs = products(rows, w_join, starts, N, width, emit, [shape(half, width, BF)] * (2 * N))
    got = [swap(out) for out in outs[::2]]
    squares = squares[0] + swap(after(squares[1], outs[-1]))
    high = lax.reduce_precision(squares, 8, 7)
    middle = lax.reduce_precision(squares - high, 8, 7)
    lines = jnp.stack([high, middle, squares - high - middle])
    lines = jnp.pad(lines, ((0, LINES - 3), (0, width - half))).astype(BF)
    sends = [jnp.concatenate([add(outs[2 * i + 1], got[i]).astype(BF), lines], axis=0) for i in range(N - 1)]
    own = add(outs[-1], got[-1])
    *sends, own = lax.optimization_barrier((*sends, own))
    terms = [along_y(sends[i], steps[i]) for i in range(N - 1)]
    total = squares + sum(jnp.sum(term[half : half + 3, :half].astype(F32), axis=0) for term in terms)
    return [own, *[term[:half] for term in terms]], total, sends


def body(
    context, w_out, residual, norm_gain, w_join, dec_state, gate_s, gate_h, gate_bias, owner, pad_mask, cotangent
):
    x, z, y, c = (lax.axis_index(a) for a in AXES)
    n_owner = N * N
    tokens, width = residual.shape
    half = tokens // 2
    slot_rows, features = dec_state.shape
    most = slot_rows // n_owner
    first = c == 0

    onehot = (owner == jnp.arange(n_owner, dtype=jnp.int32)[None, :]).astype(BF)
    ahead = jnp.tril(jnp.ones((tokens, tokens), BF), -1)
    before = jnp.dot(ahead, onehot, preferred_element_type=F32)
    rank = jnp.sum(before * onehot.astype(F32), axis=1).astype(jnp.int32)
    slots = owner[:, 0] * most + rank
    select = (slots[:, None] == jnp.arange(slot_rows, dtype=jnp.int32)[None, :]).astype(BF)

    both = jnp.concatenate([dec_state, cotangent], axis=1).reshape(n_owner, most, 2 * features)

    summed, both = project(
        context, w_out, width, lambda *others: lax.all_to_all(after(both, *others), ("x", "z"), 0, 0, tiled=True)
    )
    both = both.reshape(slot_rows, 2 * features)
    gain, mask = norm_gain[None, :], pad_mask.astype(F32)[:, None]
    residual = residual.astype(F32)
    mixed = residual + summed
    squares = jnp.sum(mixed * mixed, axis=1)
    rows = (mixed * gain * mask).astype(BF)
    rows = jnp.where(first, rows, jnp.concatenate([rows[half:], rows[:half]], axis=0))

    gated, both = lax.optimization_barrier((rows, both))
    squares = squares.reshape(2, half)
    squares = jnp.where(first, squares[0], squares[1]), jnp.where(first, squares[1], squares[0])
    terms, total, sends = join(gated, w_join, 2 * features, squares)
    rows_sent = after(rows, *sends)
    rows_1, rows_3 = along_z(rows_sent, -1), along_z(rows_sent, 1)
    hidden = add(*terms)
    scale = lax.rsqrt(total / (width * N * 2) + 1e-05)[:, None]
    both = jnp.dot(select, after(both, *sends), preferred_element_type=F32).astype(BF)
    keep = jnp.where(first, both[:half], both[half:])
    got = swap(jnp.where(first, both[half:], both[:half]))

    def widen(mine, other):
        return jnp.where(
            first, jnp.concatenate([mine, other], axis=-1), jnp.concatenate([other, mine], axis=-1)
        )

    state_t = widen(keep[:, :features], got[:, :features]).astype(F32)
    outer_t = widen(keep[:, features:], got[:, features:]).astype(F32)
    params = jnp.stack([gate_s, gate_h, gate_bias])
    params_t = widen(params, swap(params))

    hidden = (hidden * scale).astype(BF)

    def gates(params, state, hidden):
        gate = jax.nn.sigmoid(params[0][None, :] * state + params[1][None, :] * hidden + params[2][None, :])
        return gate, gate * (1.0 - gate) * hidden

    gate, slope = gates(params_t, state_t, hidden.astype(F32))
    grad = (outer_t * (gate + slope * params_t[1][None, :]) * scale).astype(BF)

    quarter = 2 * features // N

    def quarter_for(step):
        return lax.dynamic_slice_in_dim(grad, lax.rem(z + step + N, N) * quarter, quarter, 1)

    others = {f: along_z(quarter_for(-f), -f) for f in (2, 1, 3)}
    block = jnp.stack([quarter_for(0), others[1], others[2], others[3]])
    block, rows_1, rows_3 = lax.optimization_barrier((block, rows_1, rows_3))
    rows_2 = along_z(after(rows, block), 2)
    arrived = {d: along_y(block, -d) for d in (2, 1, 3)}
    arrived[1], arrived[2], arrived[3], rows_2 = lax.optimization_barrier((arrived[1], arrived[2], arrived[3], rows_2))
    pieces = [block, arrived[1], arrived[2], arrived[3]]
    swapped = [swap(piece) for piece in pieces]
    grads = jnp.stack([jnp.stack(pair, axis=1) for pair in zip(pieces, swapped)]).reshape(N, N * tokens, quarter)
    rows_z = lax.optimization_barrier(jnp.concatenate([rows, rows_1, rows_2, rows_3], axis=0))

    keep = jnp.where(first, hidden[:, :features], hidden[:, features:])
    got = swap(jnp.where(first, hidden[:, features:], hidden[:, :features]))
    rows_h = jnp.where(first, jnp.concatenate([keep, got], axis=0), jnp.concatenate([got, keep], axis=0))
    placed = lax.dot_general(select, rows_h, (((0,), (0,)), ((), ())), preferred_element_type=F32)
    placed = after(placed.astype(BF), block).reshape(n_owner, most, features)
    placed = lax.all_to_all(placed, ("x", "z"), 0, 0, tiled=True)
    placed = placed.reshape(slot_rows, features).astype(F32)

    def grad_term(step, part):
        columns = lax.dynamic_index_in_dim(grads, lax.rem(x + step - y + 2 * N, N), 0, keepdims=False)
        lines = rows_z[:, : width // 2] if part == 0 else rows_z[:, width // 2 :]
        return lax.dot_general(lines, columns, (((0,), (0,)), ((), ())), preferred_element_type=F32)

    from_left = along_x(grad_term(2, 0).astype(BF), 1)
    from_right = along_x(grad_term(2, 1).astype(BF), -1)
    near = grad_term(1, 1).astype(BF), grad_term(-1, 0).astype(BF)
    low_b, up_a = along_x(near[0], 1), along_x(near[1], -1)
    last = add(grad_term(1, 0), from_left).astype(BF), add(grad_term(-1, 1), from_right).astype(BF)
    low_a, up_b = along_x(last[0], 1), along_x(last[1], -1)
    placed = placed + from_left[0, 0] * 0.0
    state = dec_state.astype(F32)
    gate, slope = gates(params, state, placed)
    joined = (state + gate * placed).astype(BF)
    state_grad = (cotangent.astype(F32) * (1.0 + slope * gate_s[None, :])).astype(BF)
    join_grad = jnp.concatenate(
        [add(grad_term(0, 0), up_a, low_a), add(grad_term(0, 1), low_b, up_b)], axis=0
    )
    return joined, state_grad, join_grad


def solution(mesh):
    fine = Mesh(mesh.devices.reshape(N, N, N, 2), AXES)
    dp, mp = ("x", "z"), ("y", "c")
    in_specs = (
        P(dp, mp),
        P(mp, None),
        P(dp, mp),
        P(mp),
        P(mp, None),
        P(dp, mp),
        P(mp),
        P(mp),
        P(mp),
        P(dp, None),
        P(dp),
        P(dp, mp),
    )
    out_specs = (P(dp, mp), P(dp, mp), P(mp, dp))
    return jax.shard_map(body, mesh=fine, in_specs=in_specs, out_specs=out_specs, check_vma=False)
```
